32 devices in a mesh: groups: 2 (over y), seq: 4 (over z), fsdp: 4 (over x, core).
Axes of the slice: x: 2, y: 2, z: 4, core: 2. Of those that a mesh axis runs over, the one named last changes fastest.
Arguments:
- normed_layer_input: bfloat16 [1024, 8192], P(('groups', 'seq'), 'fsdp'), parts along dimension 0, may hold values from -6 to 6
- frozen_query_rows: bfloat16 [1024, 4096], P(('groups', 'seq'), 'fsdp'), parts along dimension 0, may hold values from -16 to 16
- frozen_key_rows: bfloat16 [1024, 512], P(('groups', 'seq'), 'fsdp'), parts along dimension 0, may hold values from -16 to 16
- frozen_value_rows: bfloat16 [1024, 512], P(('groups', 'seq'), 'fsdp'), parts along dimension 0, may hold values from -6 to 6
- output_gradient: bfloat16 [1024, 4096], P(('groups', 'seq'), 'fsdp'), parts along dimension 0, may hold values from -0.059814453 to 0.059814453
- segment: int32 [1024], P(('groups', 'seq')), parts along dimension 0, may hold values from 0 to 15, never falling along the last dimension, each value on 1 to 64 neighbouring positions
- adapter_down_weight: bfloat16 [8192, 32], P('fsdp'), may hold values from -0.0625 to 0.0625
- query_up_weight: bfloat16 [16, 4096], P(None, 'fsdp'), may hold values from -0.375 to 0.375
- value_up_weight: bfloat16 [16, 512], P(None, 'fsdp'), may hold values from -0.75 to 0.75
Outputs:
- grad_down: float32 [16384, 32], P(('groups', 'fsdp')), parts along dimension 0
- query_up_gradient: float32 [32, 4096], P('groups', 'fsdp'), parts along dimension 0
- value_up_gradient: float32 [32, 512], P('groups', 'fsdp'), parts along dimension 0
The draws below stay inside these ranges and needn't reach their ends.
There are 2 independent parts, one for each index of `groups`. The reference program is written for one: setup_inputs(seed, part) draws one part's arguments, and reference() takes and returns one part's arrays. A program takes and returns all parts, laid end to end along the dimension named above; an argument that names none is the same for every part. Nothing has to cross between parts.
Inputs may be any that keep to these rules, and one draw needn't show every extreme that they name: `segment`: document numbers never fall along the window; each document spans 1 to 64 consecutive tokens, and one spans exactly 64.
All inputs are finite; a program needn't handle non-finite values.
Results may differ from the reference program's by a relative error of at most 0.012.
The reference program's roundings to bfloat16 on the way count: a program that leaves them out, or rounds other values in their place, can miss the bound.
Values may be sent and summed in bfloat16 or wider, within the bound.
A program may use at most 64 MiB of HBM per device.

```python
import math
import jax
import jax.numpy as jnp
import numpy as np
from jax import lax

MODEL_WIDTH = 8192
QUERY_HEADS = 32
KEY_VALUE_HEADS = 4
HEAD_SIZE = 128
ADAPTER_RANK = 16
WINDOW_TOKENS = 512


def draw_frozen_query_rows(key, part):
    rotary_base = jnp.clip(jax.random.normal(key, (WINDOW_TOKENS, QUERY_HEADS * HEAD_SIZE), jnp.float32), -6.0, 6.0)
    return rotary_base.astype(jnp.bfloat16)


def draw_frozen_key_rows(key, part):
    rotary_base = jnp.clip(jax.random.normal(key, (WINDOW_TOKENS, KEY_VALUE_HEADS * HEAD_SIZE), jnp.float32), -6.0, 6.0)
    return rotary_base.astype(jnp.bfloat16)


def steps_of(own_key, extent, split, smallest, largest):
    def one(position, parts):
        heights = jax.random.uniform(jax.random.fold_in(jax.random.fold_in(own_key, 6), position), (parts,), jnp.float32, smallest / len(split), largest / len(split))
        return jnp.repeat(jnp.exp(heights), extent[position] // parts).reshape((-1,) + (1,) * (len(extent) - position - 1))

    gain = one(*split[0])
    for cut in split[1:]:
        gain = gain * one(*cut)
    return gain


def split_up(amount, total, limit, slope):
    loads = [(1 << 20) // math.isqrt(standing ** slope) + 1 for standing in range(2, amount + 1)]
    spare, counts = total - limit - (amount - 1), [1] * (amount - 1)
    while spare > 0:
        movable = [i for i in range(amount - 1) if counts[i] < limit]
        mass, left = sum([loads[i] for i in movable]), spare
        for i in movable:
            addition = min(limit - counts[i], max(1, left * loads[i] // mass), spare)
            counts[i] = counts[i] + addition
            spare = spare - addition
    return np.array([limit] + counts)


def ragged_sizes(rng, number_of, total, reach, slope):
    if number_of == 2:
        one = jax.random.randint(rng, (), max(1, total - reach), min(reach, total - 1) + 1)
        return jnp.stack([one, total - one])
    tallies = jnp.asarray(split_up(number_of, total, reach, slope), jnp.int32)
    couples = (number_of - 1) // 2
    donor, receiver = tallies[1:1 + 2 * couples:2], tallies[2:2 + 2 * couples:2]
    slack = jnp.minimum(donor - 1, reach - receiver)
    passed = jax.random.randint(jax.random.fold_in(rng, 1), (couples,), 0, 1 << 20) % (slack + 1)
    tallies = tallies.at[1:1 + 2 * couples:2].set(donor - passed).at[2:2 + 2 * couples:2].set(receiver + passed)
    return tallies[jax.random.permutation(jax.random.fold_in(rng, 2), number_of)]


def gaussian(stream_key, shape, spread, reach, pieces=(), held_as=jnp.bfloat16):
    values = jax.random.normal(stream_key, shape, jnp.float32) * spread
    if len(pieces) > 0:
        values = steps_of(stream_key, shape, pieces, -0.22, 0.18) * values
    return jnp.clip(values, min=-reach, max=reach).astype(held_as)


def setup_inputs(seed: int = 0, part: int = 0) -> dict:
    keys = jax.random.split(jax.random.key(seed), 10)
    part_splits = jax.random.split(jax.random.fold_in(keys[9], part), 10)
    return {
        "normed_layer_input": gaussian(part_splits[0], (WINDOW_TOKENS, MODEL_WIDTH), 1.0, 6.0, ((0, 4), (1, 4))),
        "frozen_query_rows": draw_frozen_query_rows(jax.random.fold_in(jax.random.fold_in(keys[9], part), 71), part),
        "frozen_key_rows": draw_frozen_key_rows(jax.random.fold_in(jax.random.fold_in(keys[9], part), 71), part),
        "frozen_value_rows": gaussian(part_splits[3], (WINDOW_TOKENS, KEY_VALUE_HEADS * HEAD_SIZE), 1.0, 6.0, ((0, 4), (1, 4))),
        "output_gradient": gaussian(part_splits[4], (WINDOW_TOKENS, QUERY_HEADS * HEAD_SIZE), 0.01, 0.059814453, ((0, 4), (1, 4))),
        "segment": jnp.searchsorted(jnp.cumsum(ragged_sizes(part_splits[5], max(16, WINDOW_TOKENS // 128), WINDOW_TOKENS, WINDOW_TOKENS // 8, 1)), jnp.arange(WINDOW_TOKENS), side="right").astype(jnp.int32),
        "adapter_down_weight": gaussian(keys[6], (MODEL_WIDTH, 2 * ADAPTER_RANK), MODEL_WIDTH ** -0.5, 0.0625, ((0, 4),)),
        "query_up_weight": gaussian(keys[7], (ADAPTER_RANK, QUERY_HEADS * HEAD_SIZE), (ADAPTER_RANK * 16) ** -0.5, 0.375, ((1, 4),)),
        "value_up_weight": gaussian(keys[8], (ADAPTER_RANK, KEY_VALUE_HEADS * HEAD_SIZE), (ADAPTER_RANK * 4) ** -0.5, 0.75, ((1, 4),)),
    }


ADAPTER_SCALE = 2.0
ROPE_BASE = 500000.0
NEG_FILL = -1e+30

def apply_rotation(vectors, token_positions, sign):
    half = vectors.shape[-1] // 2
    freqs = ROPE_BASE ** (-(2.0 * jnp.arange(half, dtype=jnp.float32)) / vectors.shape[-1])
    angles = token_positions.astype(jnp.float32)[:, None] * freqs[None, :]
    cosine = jnp.cos(angles)[:, None, :]
    sine = sign * jnp.sin(angles)[:, None, :]
    first = vectors[..., :half]
    second = vectors[..., half:]
    return jnp.concatenate([first * cosine - second * sine, second * cosine + first * sine], axis=-1)

def reference(normed_layer_input, frozen_query_rows, frozen_key_rows, frozen_value_rows, output_gradient, segment, adapter_down_weight, query_up_weight, value_up_weight):
    sequence_length = normed_layer_input.shape[0]
    heads_per_group = QUERY_HEADS // KEY_VALUE_HEADS
    inv_root = 1.0 / math.sqrt(HEAD_SIZE)
    adapter_product = jnp.dot(normed_layer_input, adapter_down_weight, preferred_element_type=jnp.float32).astype(jnp.bfloat16)
    query_adapter_codes = adapter_product[:, :ADAPTER_RANK]
    value_adapter_codes = adapter_product[:, ADAPTER_RANK:]
    token_positions = jnp.arange(sequence_length, dtype=jnp.int32)
    rotated_query = frozen_query_rows.astype(jnp.float32) + ADAPTER_SCALE * jnp.dot(query_adapter_codes, query_up_weight, preferred_element_type=jnp.float32)
    rotated_query = apply_rotation(rotated_query.reshape(sequence_length, QUERY_HEADS, HEAD_SIZE), token_positions, 1.0).astype(jnp.bfloat16)
    rotated_keys = apply_rotation(frozen_key_rows.astype(jnp.float32).reshape(sequence_length, KEY_VALUE_HEADS, HEAD_SIZE), token_positions, 1.0).astype(jnp.bfloat16)
    value_rows = (frozen_value_rows.astype(jnp.float32) + ADAPTER_SCALE * jnp.dot(value_adapter_codes, value_up_weight, preferred_element_type=jnp.float32)).astype(jnp.bfloat16)
    value_rows = value_rows.reshape(sequence_length, KEY_VALUE_HEADS, HEAD_SIZE)
    grads_out = output_gradient.reshape(sequence_length, QUERY_HEADS, HEAD_SIZE)
    block = math.gcd(sequence_length, 512)

    def single_group(index):
        q_group = lax.dynamic_slice_in_dim(rotated_query, index * heads_per_group, heads_per_group, 1)
        o_group = lax.dynamic_slice_in_dim(grads_out, index * heads_per_group, heads_per_group, 1)
        k_one = lax.dynamic_index_in_dim(rotated_keys, index, 1, keepdims=False)
        v_one = lax.dynamic_index_in_dim(value_rows, index, 1, keepdims=False)
        dq_parts = []
        dv_total = jnp.zeros((sequence_length, HEAD_SIZE), jnp.float32)
        for start in range(0, sequence_length, block):
            stop = start + block
            q_blk = q_group[start:stop].astype(jnp.float32)
            o_blk = o_group[start:stop].astype(jnp.float32)
            k_pre = k_one[:stop].astype(jnp.float32)
            v_pre = v_one[:stop].astype(jnp.float32)
            scores = jnp.einsum('qhd,kd->qhk', q_blk, k_pre) * inv_root
            allowed = (token_positions[:stop][None, :] <= token_positions[start:stop][:, None]) & (segment[:stop][None, :] == segment[start:stop][:, None])
            scores = jnp.where(allowed[:, None, :], scores, NEG_FILL)
            top = lax.optimization_barrier(jnp.max(scores, axis=-1, keepdims=True))
            expo = jnp.exp(scores - top)
            weights = expo / lax.optimization_barrier(jnp.sum(expo, axis=-1, keepdims=True))
            weights_b = weights.astype(jnp.bfloat16)
            dprob = jnp.einsum('qhd,kd->qhk', o_blk, v_pre)
            delta = lax.optimization_barrier(jnp.sum(weights * dprob, axis=-1, keepdims=True))
            dscore = (weights * (dprob - delta) * inv_root).astype(jnp.bfloat16)
            dq_parts.append(jnp.einsum('qhk,kd->qhd', dscore.astype(jnp.float32), k_pre))
            dv_total = dv_total.at[:stop].add(jnp.einsum('qhk,qhd->kd', weights_b.astype(jnp.float32), o_blk))
        return (jnp.concatenate(dq_parts, axis=0), dv_total)
    query_gradient_full, value_gradient_full = lax.map(single_group, jnp.arange(KEY_VALUE_HEADS, dtype=jnp.int32))
    dq = jnp.transpose(query_gradient_full, (1, 0, 2, 3)).reshape(sequence_length, QUERY_HEADS, HEAD_SIZE)
    query_gradient_rows = apply_rotation(dq, token_positions, -1.0).astype(jnp.bfloat16).reshape(sequence_length, QUERY_HEADS * HEAD_SIZE)
    value_gradient_rows = jnp.transpose(value_gradient_full, (1, 0, 2)).reshape(sequence_length, KEY_VALUE_HEADS * HEAD_SIZE)
    query_code_gradient = ADAPTER_SCALE * jnp.dot(query_gradient_rows, query_up_weight.T, preferred_element_type=jnp.float32)
    value_code_gradient = ADAPTER_SCALE * jnp.dot(value_gradient_rows, value_up_weight.astype(jnp.float32).T, precision=lax.Precision.HIGHEST)
    dlow = jnp.concatenate([query_code_gradient, value_code_gradient], axis=1).astype(jnp.bfloat16)
    grad_down = jnp.dot(normed_layer_input.T, dlow, preferred_element_type=jnp.float32)
    query_up_gradient = ADAPTER_SCALE * jnp.dot(query_adapter_codes.T, query_gradient_rows, preferred_element_type=jnp.float32)
    value_up_gradient = ADAPTER_SCALE * jnp.dot(value_adapter_codes.astype(jnp.float32).T, value_gradient_rows, precision=lax.Precision.HIGHEST)
    return (grad_down, query_up_gradient, value_up_gradient)
```

```python
import functools
import math

import jax
import jax.numpy as jnp
import numpy as np
from jax import lax
from jax.experimental import pallas as pl
from jax.experimental.pallas import tpu as pltpu
from jax.sharding import PartitionSpec as P

HEAD_SIZE = 128
ADAPTER_RANK = 16


ADAPTER_SCALE = 2.0
ROPE_BASE = 500000.0
NEG_FILL = -1e30
HIGH_PRECISION = lax.Precision.HIGHEST


def apply_rotation(vectors, token_positions, sign):
    half = vectors.shape[-1] // 2
    freqs = ROPE_BASE ** (-(2.0 * jnp.arange(half, dtype=jnp.float32)) / vectors.shape[-1])
    angles = token_positions.astype(jnp.float32)[:, None] * freqs[None, :]
    cosine = jnp.cos(angles)[:, None, :]
    sine = sign * jnp.sin(angles)[:, None, :]
    first = vectors[..., :half]
    second = vectors[..., half:]
    return jnp.concatenate(
        [first * cosine - second * sine, second * cosine + first * sine], axis=-1
    )


def contract_rows(left, right):
    return lax.dot_general(
        left, right, (((0,), (0,)), ((), ())), precision=None, preferred_element_type=jnp.float32
    )


def general_body(
    normed_layer_input,
    frozen_query_rows,
    frozen_key_rows,
    frozen_value_rows,
    output_gradient,
    segment,
    adapter_down_weight,
    query_up_weight,
    value_up_weight,
):
    tok_here = normed_layer_input.shape[0]
    seq_count = lax.axis_size("seq")
    seq_index = lax.axis_index("seq")
    heads_here = frozen_query_rows.shape[1] // HEAD_SIZE
    total = tok_here * seq_count
    longest_doc = total // 8
    inv_root = 1.0 / math.sqrt(HEAD_SIZE)
    value_partial_sum = jnp.dot(
        normed_layer_input, adapter_down_weight, preferred_element_type=jnp.float32
    )
    adapter_product = lax.psum(value_partial_sum, "fsdp").astype(jnp.bfloat16)
    query_adapter_codes = adapter_product[:, :ADAPTER_RANK]
    value_adapter_codes = adapter_product[:, ADAPTER_RANK:]
    own_pos = seq_index * tok_here + jnp.arange(tok_here, dtype=jnp.int32)
    rotated_query = frozen_query_rows.astype(jnp.float32) + ADAPTER_SCALE * jnp.dot(
        query_adapter_codes, query_up_weight, preferred_element_type=jnp.float32
    )
    rotated_query = apply_rotation(
        rotated_query.reshape(tok_here, heads_here, HEAD_SIZE), own_pos, 1.0
    ).astype(jnp.bfloat16)
    query_rows = rotated_query.reshape(tok_here * heads_here, HEAD_SIZE)
    grad_rows = output_gradient.reshape(tok_here * heads_here, HEAD_SIZE)
    keys_here = (
        apply_rotation(
            frozen_key_rows.astype(jnp.float32).reshape(tok_here, 1, HEAD_SIZE), own_pos, 1.0
        )
        .reshape(tok_here, HEAD_SIZE)
        .astype(jnp.bfloat16)
    )
    values_here = (
        frozen_value_rows.astype(jnp.float32)
        + ADAPTER_SCALE
        * jnp.dot(value_adapter_codes, value_up_weight, preferred_element_type=jnp.float32)
    ).astype(jnp.bfloat16)
    q_recv, o_recv = (
        lax.all_to_all(query_rows, "seq", split_axis=0, concat_axis=0, tiled=True),
        lax.all_to_all(grad_rows, "seq", split_axis=0, concat_axis=0, tiled=True),
    )
    keys_all, values_all, seg_all = (
        lax.all_gather(keys_here, "seq", axis=0, tiled=True),
        lax.all_gather(values_here, "seq", axis=0, tiled=True),
        lax.all_gather(segment, "seq", axis=0, tiled=True),
    )
    rows_all = tok_here * heads_here
    piece = rows_all // seq_count
    row_ids = jnp.arange(rows_all, dtype=jnp.int32)
    source = row_ids // piece
    flat = seq_index * piece + row_ids % piece
    query_pos = source * tok_here + flat // heads_here
    query_seg = jnp.take(seg_all, query_pos)
    key_pos = jnp.arange(total, dtype=jnp.int32)
    block_count = min(seq_count, 16)
    per_block = seq_count // block_count
    block_rows = per_block * piece
    dq_parts = []
    value_acc = jnp.zeros((total, HEAD_SIZE), jnp.float32)
    for block in range(block_count):
        row_lo = block * block_rows
        row_hi = row_lo + block_rows
        first_token = block * per_block * tok_here
        key_lo = max(0, first_token - longest_doc)
        key_hi = first_token + per_block * tok_here
        q_blk = q_recv[row_lo:row_hi]
        o_blk = o_recv[row_lo:row_hi]
        k_pre = keys_all[key_lo:key_hi]
        v_pre = values_all[key_lo:key_hi]
        scores = jnp.dot(q_blk, k_pre.T, preferred_element_type=jnp.float32) * inv_root
        allowed = (key_pos[key_lo:key_hi][None, :] <= query_pos[row_lo:row_hi][:, None]) & (
            seg_all[key_lo:key_hi][None, :] == query_seg[row_lo:row_hi][:, None]
        )
        scores = jnp.where(allowed, scores, NEG_FILL)
        top = jnp.max(scores, axis=-1, keepdims=True)
        expo = jnp.exp(scores - top)
        weights = expo / jnp.sum(expo, axis=-1, keepdims=True)
        weights_b = weights.astype(jnp.bfloat16)
        dprob = jnp.dot(o_blk, v_pre.T, preferred_element_type=jnp.float32)
        delta = jnp.sum(weights * dprob, axis=-1, keepdims=True)
        dscore = (weights * (dprob - delta) * inv_root).astype(jnp.bfloat16)
        dq_parts.append(jnp.dot(dscore, k_pre, preferred_element_type=jnp.float32))
        value_acc = value_acc.at[key_lo:key_hi].add(contract_rows(weights_b, o_blk))
    dq_rows = jnp.concatenate(dq_parts, axis=0)
    qgrad_rows = (
        apply_rotation(dq_rows.reshape(rows_all, 1, HEAD_SIZE), query_pos, -1.0)
        .reshape(rows_all, HEAD_SIZE)
        .astype(jnp.bfloat16)
    )
    query_gradient_local = lax.all_to_all(
        qgrad_rows, "seq", split_axis=0, concat_axis=0, tiled=True
    ).reshape(tok_here, heads_here * HEAD_SIZE)
    query_codes = ADAPTER_SCALE * jnp.dot(
        query_gradient_local, query_up_weight.T, preferred_element_type=jnp.float32
    )
    query_up_partial = ADAPTER_SCALE * jnp.dot(
        query_adapter_codes.T, query_gradient_local, preferred_element_type=jnp.float32
    )
    value_gradient_local = lax.psum_scatter(value_acc, "seq", scatter_dimension=0, tiled=True)
    value_codes = ADAPTER_SCALE * jnp.dot(
        value_gradient_local, value_up_weight.astype(jnp.float32).T, precision=HIGH_PRECISION
    )
    value_up_partial = ADAPTER_SCALE * jnp.dot(
        value_adapter_codes.astype(jnp.float32).T, value_gradient_local, precision=HIGH_PRECISION
    )
    code_q_all, code_v_all = lax.psum((query_codes, value_codes), "fsdp")
    dlow = jnp.concatenate([code_q_all, code_v_all], axis=1).astype(jnp.bfloat16)
    down_part = contract_rows(normed_layer_input, dlow)
    grad_down, query_up_gradient, value_up_gradient = lax.psum(
        (down_part, query_up_partial, value_up_partial), "seq"
    )
    return (grad_down, query_up_gradient, value_up_gradient)


def rotary_tables(total):
    half = HEAD_SIZE // 2
    freqs = ROPE_BASE ** (-(2.0 * np.arange(half, dtype=np.float64)) / HEAD_SIZE)
    angles = np.arange(total, dtype=np.float64)[:, None] * freqs[None, :]
    cosine = np.cos(angles)
    sine = np.sin(angles)
    by_row = np.concatenate([cosine, cosine, -sine, sine], axis=1).astype(np.float32)
    by_column = np.concatenate([cosine.T, sine.T], axis=0).astype(np.float32)
    return by_row, by_column


def fused_kernel(
    seq_count,
    fsdp_count,
    halo,
    x_hbm,
    fq_hbm,
    fk_hbm,
    fv_hbm,
    og_hbm,
    seg_hbm,
    down_hbm,
    qup_hbm,
    vup_hbm,
    row_table_hbm,
    col_table_hbm,
    grad_ref,
    query_up_ref,
    value_up_ref,
    x_ref,
    fq_ref,
    fk_ref,
    fv_ref,
    og_ref,
    seg_ref,
    down_ref,
    qup_ref,
    vup_ref,
    row_table_ref,
    col_table_ref,
    load_sem,
    low_buf,
    low_halo,
    keys,
    halo_keys,
    halo_frozen,
    seg_halo,
    code_buf,
    code_halo,
    code_halo_out,
    up_own,
    local_sem,
    up_in,
    up_sum,
    upv_send,
    upv_recv,
    upg_send,
    upg_recv,
    scatter_out,
    scatter_in,
    gather_own,
    gather_out,
    up_out,
    upv_out,
    low_send,
    low_recv,
    lowh_send,
    lowh_recv,
    halo_send,
    halo_recv,
    code_send,
    code_recv,
    codeh_send,
    codeh_recv,
    up_send,
    up_recv,
    rs_send,
    rs_recv,
    ag_send,
    ag_recv,
):
    group = lax.axis_index("groups")
    seq = lax.axis_index("seq")
    fsdp = lax.axis_index("fsdp")
    tokens = x_ref.shape[0]
    first_token = pl.multiple_of(seq * tokens, tokens)
    heads = fq_ref.shape[1] // HEAD_SIZE
    columns = x_ref.shape[1] // seq_count
    rank = ADAPTER_RANK
    up_columns = heads * HEAD_SIZE // seq_count
    half = HEAD_SIZE // 2
    inv_root = 1.0 / math.sqrt(HEAD_SIZE)
    f32, bf16 = jnp.float32, jnp.bfloat16
    dims_nt = (((1,), (1,)), ((), ()))
    dims_tn = (((0,), (0,)), ((), ()))
    dims_nn = (((1,), (0,)), ((), ()))

    def dot(left, right, dims, precision=None):
        return lax.dot_general(
            left, right, dims, precision=precision, preferred_element_type=f32
        )

    def remote(source, target, send, recv, to_seq, to_fsdp):
        return pltpu.make_async_remote_copy(
            src_ref=source,
            dst_ref=target,
            send_sem=send,
            recv_sem=recv,
            device_id=(group, to_seq, to_fsdp),
            device_id_type=pl.DeviceIdType.MESH,
        )

    def seq_peer(step):
        return lax.rem(seq + step, seq_count)

    def fsdp_peer(step):
        return lax.rem(fsdp + step, fsdp_count)

    has_next = seq < seq_count - 1
    has_previous = seq > 0

    loads = {}

    def load(name, source, target):
        copy = pltpu.make_async_copy(source, target, load_sem.at[len(loads)])
        copy.start()
        loads[name] = copy

    load("down", down_hbm, down_ref)
    for part in range(seq_count):
        lanes = pl.ds(part * columns, columns)
        load(part, x_hbm.at[:, lanes], x_ref.at[:, lanes])
    barrier = pltpu.get_barrier_semaphore()

    def greet(to_seq, to_fsdp):
        pl.semaphore_signal(
            barrier,
            inc=1,
            device_id=(group, to_seq, to_fsdp),
            device_id_type=pl.DeviceIdType.MESH,
        )

    for df in range(1, fsdp_count):
        greet(seq, fsdp_peer(df))

    @pl.when(has_previous)
    def _():
        for df in range(1, fsdp_count):
            greet(seq - 1, fsdp_peer(df))

    @pl.when(has_next)
    def _():
        for df in range(1, fsdp_count):
            greet(seq + 1, fsdp_peer(df))

    for ds in range(1, seq_count):
        greet(seq_peer(ds), fsdp)

    load("key", fk_hbm, fk_ref)
    load("row", row_table_hbm.at[pl.ds(first_token, tokens)], row_table_ref)
    load("value", fv_hbm, fv_ref)
    load("segment", seg_hbm, seg_ref)
    load("qup", qup_hbm, qup_ref)
    load("vup", vup_hbm, vup_ref)
    load("query", fq_hbm, fq_ref)
    load("cotangent", og_hbm, og_ref)
    load("column", col_table_hbm.at[:, pl.ds(first_token, tokens)], col_table_ref)

    loads["row"].wait()
    loads["key"].wait()
    cos_row = row_table_ref[:, :HEAD_SIZE]
    sin_row = row_table_ref[:, HEAD_SIZE:]

    def rotate(rows):
        return rows * cos_row + pltpu.roll(rows, half, 1) * sin_row

    keys[pl.ds(halo, tokens), :] = rotate(fk_ref[...].astype(f32)).astype(bf16)
    loads["down"].wait()
    partial = jnp.zeros((2 * rank, tokens), f32)
    for part in range(seq_count):
        loads[part].wait()
        lanes = slice(part * columns, (part + 1) * columns)
        partial = partial + dot(down_ref[:, lanes], x_ref[:, lanes], dims_nt)
    low_buf[fsdp] = partial
    loads["value"].wait()
    loads["segment"].wait()

    sides = has_previous.astype(jnp.int32) + has_next.astype(jnp.int32)
    pl.semaphore_wait(barrier, seq_count - 1 + (fsdp_count - 1) * (1 + sides))

    low_copies = []
    for df in range(1, fsdp_count):
        copy = remote(
            low_buf.at[fsdp], low_buf.at[fsdp], low_send.at[df], low_recv.at[df], seq, fsdp_peer(df)
        )
        copy.start()
        low_copies.append(copy)

    def low_halo_copies():
        return [
            remote(
                low_buf.at[fsdp, pl.ds(rank, rank)],
                low_halo.at[fsdp],
                lowh_send.at[df],
                lowh_recv.at[df],
                seq + 1,
                fsdp_peer(df),
            )
            for df in range(fsdp_count)
        ]

    def halo_copies():
        return [
            remote(
                keys.at[pl.ds(tokens, halo)], halo_keys, halo_send.at[0], halo_recv.at[0],
                seq + 1, fsdp,
            ),
            remote(
                fv_ref.at[pl.ds(tokens - halo, halo)], halo_frozen, halo_send.at[1],
                halo_recv.at[1], seq + 1, fsdp,
            ),
            remote(seg_ref, seg_halo, halo_send.at[2], halo_recv.at[2], seq + 1, fsdp),
        ]

    @pl.when(has_next)
    def _():
        for copy in low_halo_copies() + halo_copies():
            copy.start()

    @pl.when(jnp.logical_not(has_previous))
    def _():
        low_halo[...] = jnp.zeros_like(low_halo)
        halo_keys[...] = jnp.zeros_like(halo_keys)
        halo_frozen[...] = jnp.zeros_like(halo_frozen)
        seg_halo[...] = jnp.full(seg_halo.shape, -1, jnp.int32)

    for name in ("qup", "vup", "query", "cotangent", "column"):
        loads[name].wait()
    for copy in low_copies:
        copy.wait_recv()
    low = low_buf[0]
    for index in range(1, fsdp_count):
        low = low + low_buf[index]
    low = low.astype(bf16)
    low_q = low[:rank]
    low_v = low[rank:]

    query_add = dot(low_q, qup_ref[...], dims_tn)
    value_add = dot(low_v, vup_ref[...], dims_tn)
    values_here = (fv_ref[...].astype(f32) + ADAPTER_SCALE * value_add).astype(bf16)

    @pl.when(has_previous)
    def _():
        for copy in low_halo_copies() + halo_copies():
            copy.wait_recv()

    before = low_halo[0]
    for index in range(1, fsdp_count):
        before = before + low_halo[index]
    before = before.astype(bf16)
    before_add = dot(before, vup_ref[...], dims_tn)[tokens - halo :]
    values_before = (halo_frozen[...].astype(f32) + ADAPTER_SCALE * before_add).astype(bf16)
    values = jnp.concatenate([values_before, values_here], axis=0)
    keys[pl.ds(0, halo), :] = halo_keys[...]
    all_keys = keys[...]

    span = halo + tokens
    seg_own = seg_ref[...]
    seg_both = jnp.concatenate(
        [
            jnp.broadcast_to(seg_halo[...], (tokens, tokens)).T[tokens - halo :],
            jnp.broadcast_to(seg_own, (tokens, tokens)).T,
        ],
        axis=0,
    )
    key_row = lax.broadcasted_iota(jnp.int32, (span, tokens), 0) - halo
    query_lane = lax.broadcasted_iota(jnp.int32, (span, tokens), 1)
    allowed = (key_row <= query_lane) & (seg_both == jnp.broadcast_to(seg_own, (span, tokens)))

    cos_col = col_table_ref[:half]
    sin_col = col_table_ref[half:]
    cotangents = [og_ref[:, h * HEAD_SIZE : (h + 1) * HEAD_SIZE] for h in range(heads)]
    queries = []
    for head in range(heads):
        lanes = slice(head * HEAD_SIZE, (head + 1) * HEAD_SIZE)
        query = fq_ref[:, lanes].astype(f32) + ADAPTER_SCALE * query_add[:, lanes]
        queries.append(rotate(query).astype(bf16))
    value_grad = jnp.zeros((span, HEAD_SIZE), f32)
    code_q = jnp.zeros((rank, tokens), f32)
    query_grads = []
    batch = heads
    allowed_wide = jnp.concatenate([allowed] * batch, axis=1)
    cos_wide = jnp.concatenate([cos_col] * batch, axis=1)
    sin_wide = jnp.concatenate([sin_col] * batch, axis=1)
    for base in range(0, heads, batch):
        query = jnp.concatenate(queries[base : base + batch], axis=0)
        cotangent = jnp.concatenate(cotangents[base : base + batch], axis=0)
        scores = dot(all_keys, query, dims_nt) * inv_root
        dprob = dot(values, cotangent, dims_nt)
        scores = jnp.where(allowed_wide, scores, NEG_FILL)
        top = jnp.max(scores, axis=0, keepdims=True)
        expo = jnp.exp(scores - top)
        weights = expo * (1.0 / jnp.sum(expo, axis=0, keepdims=True))
        delta = jnp.sum(weights * dprob, axis=0, keepdims=True)
        dscore = (weights * (dprob - delta) * inv_root).astype(bf16)
        value_grad = value_grad + dot(weights.astype(bf16), cotangent, dims_nn)
        turned = dot(all_keys, dscore, dims_tn)
        first = turned[:half]
        second = turned[half:]
        query_grad = jnp.concatenate(
            [first * cos_wide + second * sin_wide, second * cos_wide - first * sin_wide], axis=0
        ).astype(bf16)
        for index in range(batch):
            head = base + index
            one = query_grad[:, index * tokens : (index + 1) * tokens]
            query_grads.append(one)
            lanes = slice(head * HEAD_SIZE, (head + 1) * HEAD_SIZE)
            code_q = code_q + dot(qup_ref[:, lanes], one, dims_nn)

    def two_terms(rows):
        high = rows.astype(bf16)
        return high, (rows - high.astype(f32)).astype(bf16)

    vup_twice = jnp.concatenate([vup_ref[...]] * 2, axis=1)
    here_high, here_low = two_terms(value_grad[halo:])
    value_before = value_grad[:halo]
    if halo < tokens:
        value_before = jnp.concatenate(
            [jnp.zeros((tokens - halo, HEAD_SIZE), f32), value_before], axis=0
        )
    before_high, before_low = two_terms(value_before)
    code_v = dot(vup_twice, jnp.concatenate([here_high, here_low], axis=1), dims_nt)
    code_buf[fsdp] = ADAPTER_SCALE * jnp.concatenate([code_q, code_v], axis=0)

    code_copies = []
    for df in range(1, fsdp_count):
        copy = remote(
            code_buf.at[fsdp], code_buf.at[fsdp], code_send.at[df], code_recv.at[df], seq,
            fsdp_peer(df),
        )
        copy.start()
        code_copies.append(copy)

    code_halo_out[...] = ADAPTER_SCALE * dot(
        vup_twice, jnp.concatenate([before_high, before_low], axis=1), dims_nt
    )

    def code_halo_copies():
        return [
            remote(
                code_halo_out, code_halo.at[fsdp], codeh_send.at[df], codeh_recv.at[df],
                seq - 1, fsdp_peer(df),
            )
            for df in range(fsdp_count)
        ]

    @pl.when(has_previous)
    def _():
        for copy in code_halo_copies():
            copy.start()

    @pl.when(jnp.logical_not(has_next))
    def _():
        code_halo[...] = jnp.zeros_like(code_halo)

    for head in range(heads):
        lanes = slice(head * HEAD_SIZE, (head + 1) * HEAD_SIZE)
        up_own[:, lanes] = (ADAPTER_SCALE * dot(low_q, query_grads[head], dims_nt)).astype(bf16)
    value_up = dot(
        jnp.concatenate([low_v, low_v, before, before], axis=1),
        jnp.concatenate([here_high, here_low, before_high, before_low], axis=0),
        dims_nn,
    )
    up_own[:, heads * HEAD_SIZE :] = (ADAPTER_SCALE * value_up).astype(bf16)
    up_copies = []
    for ds in range(1, seq_count):
        peer = seq_peer(ds)
        lanes = pl.ds(pl.multiple_of(peer * up_columns, up_columns), up_columns)
        pair = [
            remote(
                up_own.at[:, lanes], up_in.at[seq], up_send.at[ds], up_recv.at[ds], peer, fsdp
            ),
            remote(
                up_own.at[:, pl.ds(heads * HEAD_SIZE, HEAD_SIZE)], upv_out.at[seq],
                upv_send.at[ds], upv_recv.at[ds], peer, fsdp,
            ),
        ]
        for copy in pair:
            copy.start()
        up_copies.append(pair)
    own_lanes = pl.ds(pl.multiple_of(seq * up_columns, up_columns), up_columns)
    up_in[seq] = up_own[:, own_lanes]
    up_local = pltpu.make_async_copy(
        up_own.at[:, pl.ds(heads * HEAD_SIZE, HEAD_SIZE)], upv_out.at[seq], local_sem.at[0]
    )
    up_local.start()

    for copy in code_copies:
        copy.wait_recv()

    @pl.when(has_next)
    def _():
        for copy in code_halo_copies():
            copy.wait_recv()

    codes = code_buf[0]
    after = code_halo[0]
    for index in range(1, fsdp_count):
        codes = codes + code_buf[index]
        after = after + code_halo[index]
    dlow = jnp.concatenate([codes[:rank], codes[rank:] + after], axis=0).astype(bf16)

    def part_of(peer):
        lanes = pl.ds(pl.multiple_of(peer * columns, columns), columns)
        return dot(dlow, x_ref[:, lanes], dims_nn).astype(bf16)

    scatter_copies = []
    for ds in range(1, seq_count):
        peer = seq_peer(ds)
        scatter_out[ds] = part_of(peer)
        copy = remote(
            scatter_out.at[ds], scatter_in.at[seq], rs_send.at[ds], rs_recv.at[ds], peer, fsdp
        )
        copy.start()
        scatter_copies.append(copy)
    scatter_in[seq] = part_of(seq)
    for pair in up_copies:
        pair[0].wait_recv()
    up_total = up_in[0].astype(f32)
    for index in range(1, seq_count):
        up_total = up_total + up_in[index].astype(f32)
    up_sum[...] = up_total.astype(bf16)
    upg_copies = []
    for ds in range(1, seq_count):
        copy = remote(
            up_sum, up_out.at[seq], upg_send.at[ds], upg_recv.at[ds], seq_peer(ds), fsdp
        )
        copy.start()
        upg_copies.append(copy)
    upg_local = pltpu.make_async_copy(up_sum, up_out.at[seq], local_sem.at[2])
    upg_local.start()
    for copy in scatter_copies:
        copy.wait_recv()
    mine = scatter_in[0].astype(f32)
    for index in range(1, seq_count):
        mine = mine + scatter_in[index].astype(f32)
    gather_own[...] = mine.astype(bf16)
    gather_copies = []
    for ds in range(1, seq_count):
        copy = remote(
            gather_own, gather_out.at[seq], ag_send.at[ds], ag_recv.at[ds], seq_peer(ds), fsdp
        )
        copy.start()
        gather_copies.append(copy)
    gather_local = pltpu.make_async_copy(gather_own, gather_out.at[seq], local_sem.at[1])
    gather_local.start()

    for pair in up_copies:
        pair[1].wait_recv()
    for copy in upg_copies + gather_copies:
        copy.wait_recv()
    up_local.wait()
    upg_local.wait()
    gather_local.wait()
    for index in range(seq_count):
        grad_ref[:, index * columns : (index + 1) * columns] = gather_out[index].astype(f32)
        query_up_ref[:, index * up_columns : (index + 1) * up_columns] = up_out[index].astype(f32)
    upv_total = upv_out[0].astype(f32)
    for index in range(1, seq_count):
        upv_total = upv_total + upv_out[index].astype(f32)
    value_up_ref[...] = upv_total
    for copy in low_copies + code_copies + sum(up_copies, []) + upg_copies + scatter_copies + gather_copies:
        copy.wait_send()

    @pl.when(has_next)
    def _():
        for copy in low_halo_copies() + halo_copies():
            copy.wait_send()

    @pl.when(has_previous)
    def _():
        for copy in code_halo_copies():
            copy.wait_send()


def finish_kernel(grad_vmem, query_up_vmem, value_up_vmem, grad_hbm, query_up_hbm, value_up_hbm, sem):
    stores = [
        pltpu.make_async_copy(grad_vmem, grad_hbm, sem.at[0]),
        pltpu.make_async_copy(query_up_vmem, query_up_hbm, sem.at[1]),
        pltpu.make_async_copy(value_up_vmem, value_up_hbm, sem.at[2]),
    ]
    for store in stores:
        store.start()
    for store in stores:
        store.wait()


def fused_body(
    normed_layer_input,
    frozen_query_rows,
    frozen_key_rows,
    frozen_value_rows,
    output_gradient,
    segment,
    adapter_down_weight,
    query_up_weight,
    value_up_weight,
):
    seq_count = lax.axis_size("seq")
    fsdp_count = lax.axis_size("fsdp")
    tokens, width = normed_layer_input.shape
    head_lanes = frozen_query_rows.shape[1]
    total = tokens * seq_count
    halo = total // 8
    columns = width // seq_count
    codes = 2 * ADAPTER_RANK
    rank = ADAPTER_RANK
    by_row, by_column = rotary_tables(total)
    f32, bf16 = jnp.float32, jnp.bfloat16
    vmem, dma = pltpu.VMEM, pltpu.SemaphoreType.DMA
    grad, query_up, value_up = pl.pallas_call(
        functools.partial(fused_kernel, seq_count, fsdp_count, halo),
        out_shape=(
            pltpu.VMEM((codes, width), f32),
            pltpu.VMEM((rank, head_lanes), f32),
            pltpu.VMEM((rank, HEAD_SIZE), f32),
        ),
        in_specs=[pl.BlockSpec(memory_space=pltpu.HBM)] * 11,
        out_specs=(pl.BlockSpec(memory_space=pltpu.VMEM),) * 3,
        scratch_shapes=[
            vmem((tokens, width), bf16),
            vmem((tokens, head_lanes), bf16),
            vmem((tokens, HEAD_SIZE), bf16),
            vmem((tokens, HEAD_SIZE), bf16),
            vmem((tokens, head_lanes), bf16),
            vmem((1, tokens), jnp.int32),
            vmem((codes, width), bf16),
            vmem((rank, head_lanes), bf16),
            vmem((rank, HEAD_SIZE), bf16),
            vmem((tokens, 2 * HEAD_SIZE), f32),
            vmem((HEAD_SIZE, tokens), f32),
            dma((10 + seq_count,)),
            vmem((fsdp_count, codes, tokens), f32),
            vmem((fsdp_count, rank, tokens), f32),
            vmem((halo + tokens, HEAD_SIZE), bf16),
            vmem((halo, HEAD_SIZE), bf16),
            vmem((halo, HEAD_SIZE), bf16),
            vmem((1, tokens), jnp.int32),
            vmem((fsdp_count, codes, tokens), f32),
            vmem((fsdp_count, rank, tokens), f32),
            vmem((rank, tokens), f32),
            vmem((rank, head_lanes + HEAD_SIZE), bf16),
            dma((3,)),
            vmem((seq_count, rank, head_lanes // seq_count), bf16),
            vmem((rank, head_lanes // seq_count), bf16),
            dma((seq_count,)),
            dma((seq_count,)),
            dma((seq_count,)),
            dma((seq_count,)),
            vmem((seq_count, codes, columns), bf16),
            vmem((seq_count, codes, columns), bf16),
            vmem((codes, columns), bf16),
            vmem((seq_count, codes, columns), bf16),
            vmem((seq_count, rank, head_lanes // seq_count), bf16),
            vmem((seq_count, rank, HEAD_SIZE), bf16),
            dma((fsdp_count,)),
            dma((fsdp_count,)),
            dma((fsdp_count,)),
            dma((fsdp_count,)),
            dma((3,)),
            dma((3,)),
            dma((fsdp_count,)),
            dma((fsdp_count,)),
            dma((fsdp_count,)),
            dma((fsdp_count,)),
            dma((seq_count,)),
            dma((seq_count,)),
            dma((seq_count,)),
            dma((seq_count,)),
            dma((seq_count,)),
            dma((seq_count,)),
        ],
        compiler_params=pltpu.CompilerParams(
            collective_id=0, has_side_effects=True, vmem_limit_bytes=60 * 1024 * 1024
        ),
        name="adapter_backward",
    )(
        normed_layer_input,
        frozen_query_rows,
        frozen_key_rows,
        frozen_value_rows,
        output_gradient,
        segment.reshape(1, tokens),
        adapter_down_weight.T,
        query_up_weight,
        value_up_weight,
        jnp.asarray(by_row),
        jnp.asarray(by_column),
    )
    grad, query_up, value_up = pl.pallas_call(
        finish_kernel,
        out_shape=(
            jax.ShapeDtypeStruct((codes, width), f32),
            jax.ShapeDtypeStruct((rank, head_lanes), f32),
            jax.ShapeDtypeStruct((rank, HEAD_SIZE), f32),
        ),
        in_specs=[pl.BlockSpec(memory_space=pltpu.VMEM)] * 3,
        out_specs=(pl.BlockSpec(memory_space=pltpu.HBM),) * 3,
        scratch_shapes=[dma((3,))],
        compiler_params=pltpu.CompilerParams(vmem_limit_bytes=8 * 1024 * 1024),
        name="finish",
    )(grad, query_up, value_up)
    return grad.T, query_up, value_up


def body(*args):
    tokens = args[0].shape[0]
    seq_count = lax.axis_size("seq")
    halo = tokens * seq_count // 8
    one_back = halo <= tokens and halo % 16 == 0 and tokens == HEAD_SIZE and seq_count <= 8
    even = all(args[i].shape[1] % (seq_count * HEAD_SIZE) == 0 for i in (0, 1))
    return fused_body(*args) if one_back and even else general_body(*args)


def solution(mesh):
    in_specs = (
        P(("groups", "seq"), "fsdp"),
        P(("groups", "seq"), "fsdp"),
        P(("groups", "seq"), "fsdp"),
        P(("groups", "seq"), "fsdp"),
        P(("groups", "seq"), "fsdp"),
        P(("groups", "seq")),
        P("fsdp", None),
        P(None, "fsdp"),
        P(None, "fsdp"),
    )
    out_specs = (P(("groups", "fsdp"), None), P("groups", "fsdp"), P("groups", "fsdp"))
    return jax.shard_map(body, mesh=mesh, in_specs=in_specs, out_specs=out_specs, check_vma=False)
```

```python
import functools
import math

import jax
import jax.numpy as jnp
import numpy as np
from jax import lax
from jax.experimental import pallas as pl
from jax.experimental.pallas import tpu as pltpu
from jax.sharding import PartitionSpec as P

HEAD_SIZE = 128
ADAPTER_RANK = 16


ADAPTER_SCALE = 2.0
ROPE_BASE = 500000.0
NEG_FILL = -1e30
HIGH_PRECISION = lax.Precision.HIGHEST


def apply_rotation(vectors, token_positions, sign):
    half = vectors.shape[-1] // 2
    freqs = ROPE_BASE ** (-(2.0 * jnp.arange(half, dtype=jnp.float32)) / vectors.shape[-1])
    angles = token_positions.astype(jnp.float32)[:, None] * freqs[None, :]
    cosine = jnp.cos(angles)[:, None, :]
    sine = sign * jnp.sin(angles)[:, None, :]
    first = vectors[..., :half]
    second = vectors[..., half:]
    return jnp.concatenate(
        [first * cosine - second * sine, second * cosine + first * sine], axis=-1
    )


def contract_rows(left, right):
    return lax.dot_general(
        left, right, (((0,), (0,)), ((), ())), precision=None, preferred_element_type=jnp.float32
    )


def general_body(
    normed_layer_input,
    frozen_query_rows,
    frozen_key_rows,
    frozen_value_rows,
    output_gradient,
    segment,
    adapter_down_weight,
    query_up_weight,
    value_up_weight,
):
    tok_here = normed_layer_input.shape[0]
    seq_count = lax.axis_size("seq")
    seq_index = lax.axis_index("seq")
    heads_here = frozen_query_rows.shape[1] // HEAD_SIZE
    total = tok_here * seq_count
    longest_doc = total // 8
    inv_root = 1.0 / math.sqrt(HEAD_SIZE)
    value_partial_sum = jnp.dot(
        normed_layer_input, adapter_down_weight, preferred_element_type=jnp.float32
    )
    adapter_product = lax.psum(value_partial_sum, "fsdp").astype(jnp.bfloat16)
    query_adapter_codes = adapter_product[:, :ADAPTER_RANK]
    value_adapter_codes = adapter_product[:, ADAPTER_RANK:]
    own_pos = seq_index * tok_here + jnp.arange(tok_here, dtype=jnp.int32)
    rotated_query = frozen_query_rows.astype(jnp.float32) + ADAPTER_SCALE * jnp.dot(
        query_adapter_codes, query_up_weight, preferred_element_type=jnp.float32
    )
    rotated_query = apply_rotation(
        rotated_query.reshape(tok_here, heads_here, HEAD_SIZE), own_pos, 1.0
    ).astype(jnp.bfloat16)
    query_rows = rotated_query.reshape(tok_here * heads_here, HEAD_SIZE)
    grad_rows = output_gradient.reshape(tok_here * heads_here, HEAD_SIZE)
    keys_here = (
        apply_rotation(
            frozen_key_rows.astype(jnp.float32).reshape(tok_here, 1, HEAD_SIZE), own_pos, 1.0
        )
        .reshape(tok_here, HEAD_SIZE)
        .astype(jnp.bfloat16)
    )
    values_here = (
        frozen_value_rows.astype(jnp.float32)
        + ADAPTER_SCALE
        * jnp.dot(value_adapter_codes, value_up_weight, preferred_element_type=jnp.float32)
    ).astype(jnp.bfloat16)
    q_recv, o_recv = (
        lax.all_to_all(query_rows, "seq", split_axis=0, concat_axis=0, tiled=True),
        lax.all_to_all(grad_rows, "seq", split_axis=0, concat_axis=0, tiled=True),
    )
    keys_all, values_all, seg_all = (
        lax.all_gather(keys_here, "seq", axis=0, tiled=True),
        lax.all_gather(values_here, "seq", axis=0, tiled=True),
        lax.all_gather(segment, "seq", axis=0, tiled=True),
    )
    rows_all = tok_here * heads_here
    piece = rows_all // seq_count
    row_ids = jnp.arange(rows_all, dtype=jnp.int32)
    source = row_ids // piece
    flat = seq_index * piece + row_ids % piece
    query_pos = source * tok_here + flat // heads_here
    query_seg = jnp.take(seg_all, query_pos)
    key_pos = jnp.arange(total, dtype=jnp.int32)
    block_count = min(seq_count, 16)
    per_block = seq_count // block_count
    block_rows = per_block * piece
    dq_parts = []
    value_acc = jnp.zeros((total, HEAD_SIZE), jnp.float32)
    for block in range(block_count):
        row_lo = block * block_rows
        row_hi = row_lo + block_rows
        first_token = block * per_block * tok_here
        key_lo = max(0, first_token - longest_doc)
        key_hi = first_token + per_block * tok_here
        q_blk = q_recv[row_lo:row_hi]
        o_blk = o_recv[row_lo:row_hi]
        k_pre = keys_all[key_lo:key_hi]
        v_pre = values_all[key_lo:key_hi]
        scores = jnp.dot(q_blk, k_pre.T, preferred_element_type=jnp.float32) * inv_root
        allowed = (key_pos[key_lo:key_hi][None, :] <= query_pos[row_lo:row_hi][:, None]) & (
            seg_all[key_lo:key_hi][None, :] == query_seg[row_lo:row_hi][:, None]
        )
        scores = jnp.where(allowed, scores, NEG_FILL)
        top = jnp.max(scores, axis=-1, keepdims=True)
        expo = jnp.exp(scores - top)
        weights = expo / jnp.sum(expo, axis=-1, keepdims=True)
        weights_b = weights.astype(jnp.bfloat16)
        dprob = jnp.dot(o_blk, v_pre.T, preferred_element_type=jnp.float32)
        delta = jnp.sum(weights * dprob, axis=-1, keepdims=True)
        dscore = (weights * (dprob - delta) * inv_root).astype(jnp.bfloat16)
        dq_parts.append(jnp.dot(dscore, k_pre, preferred_element_type=jnp.float32))
        value_acc = value_acc.at[key_lo:key_hi].add(contract_rows(weights_b, o_blk))
    dq_rows = jnp.concatenate(dq_parts, axis=0)
    qgrad_rows = (
        apply_rotation(dq_rows.reshape(rows_all, 1, HEAD_SIZE), query_pos, -1.0)
        .reshape(rows_all, HEAD_SIZE)
        .astype(jnp.bfloat16)
    )
    query_gradient_local = lax.all_to_all(
        qgrad_rows, "seq", split_axis=0, concat_axis=0, tiled=True
    ).reshape(tok_here, heads_here * HEAD_SIZE)
    query_codes = ADAPTER_SCALE * jnp.dot(
        query_gradient_local, query_up_weight.T, preferred_element_type=jnp.float32
    )
    query_up_partial = ADAPTER_SCALE * jnp.dot(
        query_adapter_codes.T, query_gradient_local, preferred_element_type=jnp.float32
    )
    value_gradient_local = lax.psum_scatter(value_acc, "seq", scatter_dimension=0, tiled=True)
    value_codes = ADAPTER_SCALE * jnp.dot(
        value_gradient_local, value_up_weight.astype(jnp.float32).T, precision=HIGH_PRECISION
    )
    value_up_partial = ADAPTER_SCALE * jnp.dot(
        value_adapter_codes.astype(jnp.float32).T, value_gradient_local, precision=HIGH_PRECISION
    )
    code_q_all, code_v_all = lax.psum((query_codes, value_codes), "fsdp")
    dlow = jnp.concatenate([code_q_all, code_v_all], axis=1).astype(jnp.bfloat16)
    down_part = contract_rows(normed_layer_input, dlow)
    grad_down, query_up_gradient, value_up_gradient = lax.psum(
        (down_part, query_up_partial, value_up_partial), "seq"
    )
    return (grad_down, query_up_gradient, value_up_gradient)


def rotary_tables(total):
    half = HEAD_SIZE // 2
    freqs = ROPE_BASE ** (-(2.0 * np.arange(half, dtype=np.float64)) / HEAD_SIZE)
    angles = np.arange(total, dtype=np.float64)[:, None] * freqs[None, :]
    cosine = np.cos(angles)
    sine = np.sin(angles)
    by_row = np.concatenate([cosine, cosine, -sine, sine], axis=1).astype(np.float32)
    by_column = np.concatenate([cosine.T, sine.T], axis=0).astype(np.float32)
    return by_row, by_column


def fused_kernel(
    halo,
    x_hbm,
    fq_hbm,
    fk_hbm,
    fv_hbm,
    og_hbm,
    seg_hbm,
    down_hbm,
    qup_hbm,
    vup_hbm,
    row_table_hbm,
    col_table_hbm,
    grad_ref,
    query_up_ref,
    value_up_ref,
    x_ref,
    fq_ref,
    fk_ref,
    fv_ref,
    og_ref,
    seg_ref,
    down_ref,
    qup_ref,
    vup_ref,
    row_table_ref,
    col_table_ref,
    load_sem,
    low_buf,
    low_halo,
    keys,
    halo_frozen,
    seg_halo,
    code_v_buf,
    code_q_buf,
    code_halo,
    code_halo_out,
    up_part,
    up_in,
    up_gather,
    v_part,
    v_in,
    v_gather,
    q_part,
    q_in,
    q_gather,
    low_send,
    low_recv,
    lowh_send,
    lowh_recv,
    halo_send,
    halo_recv,
    code_v_send,
    code_v_recv,
    code_q_send,
    code_q_recv,
    codeh_send,
    codeh_recv,
    up_send,
    up_recv,
    upg_send,
    upg_recv,
    v_send,
    v_recv,
    vg_send,
    vg_recv,
    q_send,
    q_recv,
    qg_send,
    qg_recv,
):
    group = lax.axis_index("groups")
    seq = lax.axis_index("seq")
    fsdp = lax.axis_index("fsdp")
    tokens, width = x_ref.shape
    first_token = pl.multiple_of(seq * tokens, tokens)
    heads = fq_ref.shape[1] // HEAD_SIZE
    rank = ADAPTER_RANK
    wide = width // 2
    up_wide = heads * HEAD_SIZE // 2
    half = HEAD_SIZE // 2
    inv_root = 1.0 / math.sqrt(HEAD_SIZE)
    f32, bf16 = jnp.float32, jnp.bfloat16
    dims_nt = (((1,), (1,)), ((), ()))
    dims_tn = (((0,), (0,)), ((), ()))
    dims_nn = (((1,), (0,)), ((), ()))

    def dot(left, right, dims, precision=None):
        return lax.dot_general(
            left, right, dims, precision=precision, preferred_element_type=f32
        )

    def remote(source, target, send, recv, to_seq, to_fsdp):
        return pltpu.make_async_remote_copy(
            src_ref=source,
            dst_ref=target,
            send_sem=send,
            recv_sem=recv,
            device_id=(group, to_seq, to_fsdp),
            device_id_type=pl.DeviceIdType.MESH,
        )

    has_next = seq < 3
    has_previous = seq > 0
    inner = (seq == 1) | (seq == 2)
    outer = (seq == 0) | (seq == 3)
    lower = seq < 2
    owner_across = jnp.where(lower, 2, 1)
    owner_here = 3 - owner_across
    half_across = owner_across - 1
    half_here = owner_here - 1
    edge_here = jnp.where(lower, 0, 3)
    edge_across = 3 - edge_here

    loads = {}

    def load(name, source, target):
        copy = pltpu.make_async_copy(source, target, load_sem.at[len(loads)])
        copy.start()
        loads[name] = copy

    columns = width // 4
    load("down", down_hbm, down_ref)
    for part in range(4):
        lanes = pl.ds(part * columns, columns)
        load(part, x_hbm.at[:, lanes], x_ref.at[:, lanes])
    barrier = pltpu.get_barrier_semaphore()

    def greet(to_seq, to_fsdp):
        pl.semaphore_signal(
            barrier,
            inc=1,
            device_id=(group, to_seq, to_fsdp),
            device_id_type=pl.DeviceIdType.MESH,
        )

    for df in (2, 3):
        greet(seq, fsdp ^ df)

    @pl.when(has_previous)
    def _():
        for df in (2, 3, 0, 1):
            greet(seq - 1, fsdp ^ df)

    greet(seq ^ 2, fsdp)
    greet(seq, fsdp ^ 1)

    load("row", row_table_hbm.at[pl.ds(first_token, tokens)], row_table_ref)
    load("key", fk_hbm, fk_ref)
    load("value", fv_hbm, fv_ref)
    load("segment", seg_hbm, seg_ref)
    load("qup", qup_hbm, qup_ref)
    load("query", fq_hbm, fq_ref)
    load("vup", vup_hbm, vup_ref)
    load("cotangent", og_hbm, og_ref)
    load("column", col_table_hbm.at[:, pl.ds(first_token, tokens)], col_table_ref)

    loads["down"].wait()
    partial = jnp.zeros((2 * rank, tokens), f32)
    for part in range(4):
        loads[part].wait()
        lanes = slice(part * columns, (part + 1) * columns)
        partial = partial + dot(down_ref[:, lanes], x_ref[:, lanes], dims_nt)
    low_buf[0] = partial

    pl.semaphore_wait(barrier, 4 + 4 * has_next.astype(jnp.int32))

    low_copies = {}

    def low_copy(df):
        copy = remote(
            low_buf.at[0], low_buf.at[df], low_send.at[df], low_recv.at[df], seq, fsdp ^ df
        )
        copy.start()
        low_copies[df] = copy

    def low_halo_copies():
        return [
            remote(
                low_buf.at[0, pl.ds(rank, rank)],
                low_halo.at[df],
                lowh_send.at[df],
                lowh_recv.at[df],
                seq + 1,
                fsdp ^ df,
            )
            for df in (2, 3, 0, 1)
        ]

    def halo_copies():
        return [
            remote(
                keys.at[pl.ds(tokens, halo)], keys.at[pl.ds(0, halo)], halo_send.at[0],
                halo_recv.at[0], seq + 1, fsdp,
            ),
            remote(
                fv_ref.at[pl.ds(tokens - halo, halo)], halo_frozen, halo_send.at[1],
                halo_recv.at[1], seq + 1, fsdp,
            ),
            remote(seg_ref, seg_halo, halo_send.at[2], halo_recv.at[2], seq + 1, fsdp),
        ]

    low_copy(2)
    low_copy(3)

    @pl.when(has_next)
    def _():
        for copy in low_halo_copies():
            copy.start()

    low_copy(1)

    loads["row"].wait()
    loads["key"].wait()
    cos_row = row_table_ref[:, :HEAD_SIZE]
    sin_row = row_table_ref[:, HEAD_SIZE:]

    def rotate(rows):
        return rows * cos_row + pltpu.roll(rows, half, 1) * sin_row

    keys[pl.ds(halo, tokens), :] = rotate(fk_ref[...].astype(f32)).astype(bf16)
    loads["value"].wait()
    loads["segment"].wait()

    @pl.when(has_next)
    def _():
        for copy in halo_copies():
            copy.start()

    @pl.when(jnp.logical_not(has_previous))
    def _():
        low_halo[...] = jnp.zeros_like(low_halo)
        keys[pl.ds(0, halo), :] = jnp.zeros((halo, HEAD_SIZE), bf16)
        halo_frozen[...] = jnp.zeros_like(halo_frozen)
        seg_halo[...] = jnp.full(seg_halo.shape, -1, jnp.int32)

    @pl.when(jnp.logical_not(has_next))
    def _():
        code_halo[...] = jnp.zeros_like(code_halo)

    for name in ("qup", "vup", "query", "cotangent", "column"):
        loads[name].wait()

    cos_col = col_table_ref[:half]
    sin_col = col_table_ref[half:]
    cos_wide = jnp.concatenate([cos_col] * heads, axis=1)
    sin_wide = jnp.concatenate([sin_col] * heads, axis=1)
    cotangent = jnp.concatenate(
        [og_ref[:, h * HEAD_SIZE : (h + 1) * HEAD_SIZE] for h in range(heads)], axis=0
    )

    @pl.when(has_previous)
    def _():
        for copy in halo_copies():
            copy.wait_recv()

    span = halo + tokens
    seg_own = seg_ref[...]
    seg_both = jnp.concatenate(
        [
            jnp.broadcast_to(seg_halo[...], (tokens, tokens)).T[tokens - halo :],
            jnp.broadcast_to(seg_own, (tokens, tokens)).T,
        ],
        axis=0,
    )
    key_row = lax.broadcasted_iota(jnp.int32, (span, tokens), 0) - halo
    query_lane = lax.broadcasted_iota(jnp.int32, (span, tokens), 1)
    allowed = (key_row <= query_lane) & (seg_both == jnp.broadcast_to(seg_own, (span, tokens)))
    allowed_wide = jnp.concatenate([allowed] * heads, axis=1)
    all_keys = keys[...]

    for df in (1, 2, 3):
        low_copies[df].wait_recv()
    low = low_buf[fsdp]
    for index in range(1, 4):
        low = low + low_buf[fsdp ^ index]
    low = low.astype(bf16)
    low_q = low[:rank]
    low_v = low[rank:]

    query_add = dot(low_q, qup_ref[...], dims_tn)
    queries = []
    for head in range(heads):
        lanes = slice(head * HEAD_SIZE, (head + 1) * HEAD_SIZE)
        query = fq_ref[:, lanes].astype(f32) + ADAPTER_SCALE * query_add[:, lanes]
        queries.append(rotate(query).astype(bf16))
    query = jnp.concatenate(queries, axis=0)
    scores = dot(all_keys, query, dims_nt) * inv_root
    scores = jnp.where(allowed_wide, scores, NEG_FILL)
    top = jnp.max(scores, axis=0, keepdims=True)
    expo = jnp.exp(scores - top)
    weights = expo * (1.0 / jnp.sum(expo, axis=0, keepdims=True))
    value_grad = dot(weights.astype(bf16), cotangent, dims_nn)

    def two_terms(rows):
        high = rows.astype(bf16)
        return high, (rows - high.astype(f32)).astype(bf16)

    vup_twice = jnp.concatenate([vup_ref[...]] * 2, axis=1)
    here_high, here_low = two_terms(value_grad[halo:])
    value_before = value_grad[:halo]
    if halo < tokens:
        value_before = jnp.concatenate(
            [jnp.zeros((tokens - halo, HEAD_SIZE), f32), value_before], axis=0
        )
    before_high, before_low = two_terms(value_before)
    code_halo_out[...] = ADAPTER_SCALE * dot(
        vup_twice, jnp.concatenate([before_high, before_low], axis=1), dims_nt
    )
    code_v_buf[0] = ADAPTER_SCALE * dot(
        vup_twice, jnp.concatenate([here_high, here_low], axis=1), dims_nt
    )

    @pl.when(has_previous)
    def _():
        for copy in low_halo_copies():
            copy.wait_recv()

    def code_halo_copies():
        return [
            remote(
                code_halo_out, code_halo.at[df], codeh_send.at[df], codeh_recv.at[df],
                seq - 1, fsdp ^ df,
            )
            for df in (2, 3, 0, 1)
        ]

    def code_copies(buffer, send, recv):
        return [
            remote(buffer.at[0], buffer.at[df], send.at[df], recv.at[df], seq, fsdp ^ df)
            for df in (2, 3, 1)
        ]

    @pl.when(has_previous)
    def _():
        for copy in code_halo_copies():
            copy.start()

    code_v_copies = code_copies(code_v_buf, code_v_send, code_v_recv)
    for copy in code_v_copies:
        copy.start()

    value_add = dot(low_v, vup_ref[...], dims_tn)
    values_here = (fv_ref[...].astype(f32) + ADAPTER_SCALE * value_add).astype(bf16)
    before = low_halo[fsdp]
    for index in range(1, 4):
        before = before + low_halo[fsdp ^ index]
    before = before.astype(bf16)
    before_add = dot(before, vup_ref[...], dims_tn)[tokens - halo :]
    values_before = (halo_frozen[...].astype(f32) + ADAPTER_SCALE * before_add).astype(bf16)
    values = jnp.concatenate([values_before, values_here], axis=0)
    dprob = dot(values, cotangent, dims_nt)
    delta = jnp.sum(weights * dprob, axis=0, keepdims=True)
    dscore = (weights * (dprob - delta) * inv_root).astype(bf16)
    turned = dot(all_keys, dscore, dims_tn)
    first = turned[:half]
    second = turned[half:]
    query_grad = jnp.concatenate(
        [first * cos_wide + second * sin_wide, second * cos_wide - first * sin_wide], axis=0
    ).astype(bf16)
    query_grads = [query_grad[:, h * tokens : (h + 1) * tokens] for h in range(heads)]
    code_q = jnp.zeros((rank, tokens), f32)
    for head in range(heads):
        lanes = slice(head * HEAD_SIZE, (head + 1) * HEAD_SIZE)
        code_q = code_q + dot(qup_ref[:, lanes], query_grads[head], dims_nn)
    code_q_buf[0] = ADAPTER_SCALE * code_q
    code_q_copies = code_copies(code_q_buf, code_q_send, code_q_recv)
    for copy in code_q_copies:
        copy.start()

    def sums(parts, arrived, gathered, send, recv, gather_send, gather_recv):
        def across():
            return remote(
                parts.at[half_across], arrived.at[0], send.at[0], recv.at[0], owner_across, fsdp
            )

        def between():
            return remote(
                parts.at[half_across], arrived.at[1], send.at[1], recv.at[1], owner_across, fsdp
            )

        def near():
            return remote(
                parts.at[half_here], arrived.at[2], send.at[2], recv.at[2], owner_here, fsdp
            )

        mine = gathered.at[half_here]

        def spread():
            return [
                remote(mine, mine, gather_send.at[0], gather_recv.at[0], edge_across, fsdp),
                remote(mine, mine, gather_send.at[1], gather_recv.at[1], owner_across, fsdp),
                remote(mine, mine, gather_send.at[2], gather_recv.at[2], edge_here, fsdp),
            ]

        def send_across():
            @pl.when(outer)
            def _():
                across().start()

            @pl.when(inner)
            def _():
                between().start()

        def send_near():
            @pl.when(outer)
            def _():
                near().start()

        def add_and_spread():
            @pl.when(inner)
            def _():
                across().wait_recv()
                between().wait_recv()
                near().wait_recv()
                total = parts[half_here].astype(f32)
                for index in range(3):
                    total = total + arrived[index].astype(f32)
                gathered[half_here] = total.astype(bf16)
                for copy in spread():
                    copy.start()

        def wait_gathered():
            @pl.when(inner)
            def _():
                spread()[1].wait_recv()

            @pl.when(outer)
            def _():
                spread()[0].wait_recv()
                spread()[2].wait_recv()

        def wait_sent():
            @pl.when(outer)
            def _():
                across().wait_send()
                near().wait_send()

            @pl.when(inner)
            def _():
                between().wait_send()
                for copy in spread():
                    copy.wait_send()

        return send_across, send_near, add_and_spread, wait_gathered, wait_sent

    up_sums = sums(up_part, up_in, up_gather, up_send, up_recv, upg_send, upg_recv)
    v_sums = sums(v_part, v_in, v_gather, v_send, v_recv, vg_send, vg_recv)
    q_sums = sums(q_part, q_in, q_gather, q_send, q_recv, qg_send, qg_recv)

    for head in range(heads):
        side, place = divmod(head, heads // 2)
        lanes = slice(place * HEAD_SIZE, (place + 1) * HEAD_SIZE)
        up_part[side, :, lanes] = (ADAPTER_SCALE * dot(low_q, query_grads[head], dims_nt)).astype(
            bf16
        )
    value_up = dot(
        jnp.concatenate([low_v, low_v, before, before], axis=1),
        jnp.concatenate([here_high, here_low, before_high, before_low], axis=0),
        dims_nn,
    )
    value_up = (ADAPTER_SCALE * value_up).astype(bf16)
    for side in range(2):
        up_part[side, :, up_wide:] = value_up
    up_sums[0]()
    up_sums[1]()

    def part_of(dlow, side):
        lanes = pl.ds(pl.multiple_of(side * wide, wide), wide)
        return dot(dlow, x_ref[:, lanes], dims_nn).astype(bf16)

    for copy in code_v_copies:
        copy.wait_recv()

    @pl.when(has_next)
    def _():
        for copy in code_halo_copies():
            copy.wait_recv()

    codes = code_v_buf[fsdp]
    after = code_halo[fsdp]
    for index in range(1, 4):
        codes = codes + code_v_buf[fsdp ^ index]
        after = after + code_halo[fsdp ^ index]
    dlow_v = (codes + after).astype(bf16)
    v_part[half_across] = part_of(dlow_v, half_across)
    v_sums[0]()
    v_part[half_here] = part_of(dlow_v, half_here)
    v_sums[1]()
    for copy in code_q_copies:
        copy.wait_recv()
    codes = code_q_buf[fsdp]
    for index in range(1, 4):
        codes = codes + code_q_buf[fsdp ^ index]
    dlow_q = codes.astype(bf16)
    q_part[half_across] = part_of(dlow_q, half_across)
    q_sums[0]()
    q_part[half_here] = part_of(dlow_q, half_here)
    q_sums[1]()

    up_sums[2]()
    v_sums[2]()
    q_sums[2]()

    up_sums[3]()
    for side in range(2):
        query_up_ref[:, side * up_wide : (side + 1) * up_wide] = up_gather[
            side, :, :up_wide
        ].astype(f32)
    value_up_ref[...] = up_gather[0, :, up_wide:].astype(f32)
    v_sums[3]()
    for side in range(2):
        grad_ref[rank:, side * wide : (side + 1) * wide] = v_gather[side].astype(f32)
    q_sums[3]()
    for side in range(2):
        grad_ref[:rank, side * wide : (side + 1) * wide] = q_gather[side].astype(f32)

    for copy in list(low_copies.values()) + code_v_copies + code_q_copies:
        copy.wait_send()
    for group_sums in (up_sums, v_sums, q_sums):
        group_sums[4]()

    @pl.when(has_next)
    def _():
        for copy in low_halo_copies() + halo_copies():
            copy.wait_send()

    @pl.when(has_previous)
    def _():
        for copy in code_halo_copies():
            copy.wait_send()


def finish_kernel(grad_vmem, query_up_vmem, value_up_vmem, grad_hbm, query_up_hbm, value_up_hbm, sem):
    stores = [
        pltpu.make_async_copy(grad_vmem, grad_hbm, sem.at[0]),
        pltpu.make_async_copy(query_up_vmem, query_up_hbm, sem.at[1]),
        pltpu.make_async_copy(value_up_vmem, value_up_hbm, sem.at[2]),
    ]
    for store in stores:
        store.start()
    for store in stores:
        store.wait()


def fused_body(
    normed_layer_input,
    frozen_query_rows,
    frozen_key_rows,
    frozen_value_rows,
    output_gradient,
    segment,
    adapter_down_weight,
    query_up_weight,
    value_up_weight,
):
    tokens, width = normed_layer_input.shape
    head_lanes = frozen_query_rows.shape[1]
    total = tokens * lax.axis_size("seq")
    halo = total // 8
    codes = 2 * ADAPTER_RANK
    rank = ADAPTER_RANK
    wide = width // 2
    up_lanes = head_lanes // 2 + HEAD_SIZE
    by_row, by_column = rotary_tables(total)
    f32, bf16 = jnp.float32, jnp.bfloat16
    vmem, dma = pltpu.VMEM, pltpu.SemaphoreType.DMA
    grad, query_up, value_up = pl.pallas_call(
        functools.partial(fused_kernel, halo),
        out_shape=(
            vmem((codes, width), f32),
            vmem((rank, head_lanes), f32),
            vmem((rank, HEAD_SIZE), f32),
        ),
        in_specs=[pl.BlockSpec(memory_space=pltpu.HBM)] * 11,
        out_specs=(pl.BlockSpec(memory_space=pltpu.VMEM),) * 3,
        scratch_shapes=[
            vmem((tokens, width), bf16),
            vmem((tokens, head_lanes), bf16),
            vmem((tokens, HEAD_SIZE), bf16),
            vmem((tokens, HEAD_SIZE), bf16),
            vmem((tokens, head_lanes), bf16),
            vmem((1, tokens), jnp.int32),
            vmem((codes, width), bf16),
            vmem((rank, head_lanes), bf16),
            vmem((rank, HEAD_SIZE), bf16),
            vmem((tokens, 2 * HEAD_SIZE), f32),
            vmem((HEAD_SIZE, tokens), f32),
            dma((14,)),
            vmem((4, codes, tokens), f32),
            vmem((4, rank, tokens), f32),
            vmem((halo + tokens, HEAD_SIZE), bf16),
            vmem((halo, HEAD_SIZE), bf16),
            vmem((1, tokens), jnp.int32),
            vmem((4, rank, tokens), f32),
            vmem((4, rank, tokens), f32),
            vmem((4, rank, tokens), f32),
            vmem((rank, tokens), f32),
            vmem((2, rank, up_lanes), bf16),
            vmem((3, rank, up_lanes), bf16),
            vmem((2, rank, up_lanes), bf16),
            vmem((2, rank, wide), bf16),
            vmem((3, rank, wide), bf16),
            vmem((2, rank, wide), bf16),
            vmem((2, rank, wide), bf16),
            vmem((3, rank, wide), bf16),
            vmem((2, rank, wide), bf16),
        ]
        + [dma((4,))] * 4
        + [dma((3,))] * 2
        + [dma((4,))] * 6
        + [dma((3,))] * 12,
        compiler_params=pltpu.CompilerParams(
            collective_id=0, has_side_effects=True, vmem_limit_bytes=60 * 1024 * 1024
        ),
        name="adapter_backward",
    )(
        normed_layer_input,
        frozen_query_rows,
        frozen_key_rows,
        frozen_value_rows,
        output_gradient,
        segment.reshape(1, tokens),
        adapter_down_weight.T,
        query_up_weight,
        value_up_weight,
        jnp.asarray(by_row),
        jnp.asarray(by_column),
    )
    grad, query_up, value_up = pl.pallas_call(
        finish_kernel,
        out_shape=(
            jax.ShapeDtypeStruct((codes, width), f32),
            jax.ShapeDtypeStruct((rank, head_lanes), f32),
            jax.ShapeDtypeStruct((rank, HEAD_SIZE), f32),
        ),
        in_specs=[pl.BlockSpec(memory_space=pltpu.VMEM)] * 3,
        out_specs=(pl.BlockSpec(memory_space=pltpu.HBM),) * 3,
        scratch_shapes=[dma((3,))],
        compiler_params=pltpu.CompilerParams(vmem_limit_bytes=8 * 1024 * 1024),
        name="finish",
    )(grad, query_up, value_up)
    return grad.T, query_up, value_up


def body(*args):
    tokens = args[0].shape[0]
    halo = tokens * lax.axis_size("seq") // 8
    four = lax.axis_size("seq") == 4 and lax.axis_size("fsdp") == 4
    one_back = halo <= tokens and halo % 16 == 0 and tokens == HEAD_SIZE
    even = all(args[i].shape[1] % (4 * HEAD_SIZE) == 0 for i in (0, 1))
    return fused_body(*args) if four and one_back and even else general_body(*args)


def solution(mesh):
    in_specs = (
        P(("groups", "seq"), "fsdp"),
        P(("groups", "seq"), "fsdp"),
        P(("groups", "seq"), "fsdp"),
        P(("groups", "seq"), "fsdp"),
        P(("groups", "seq"), "fsdp"),
        P(("groups", "seq")),
        P("fsdp", None),
        P(None, "fsdp"),
        P(None, "fsdp"),
    )
    out_specs = (P(("groups", "fsdp"), None), P("groups", "fsdp"), P("groups", "fsdp"))
    return jax.shard_map(body, mesh=mesh, in_specs=in_specs, out_specs=out_specs, check_vma=False)
```
